32 devices in a mesh: dp: 4 (over z), ctx: 8 (over y, x, core).
Axes of the slice: x: 2, y: 2, z: 4, core: 2. Of those that a mesh axis runs over, the one named last changes fastest.
Arguments:
- features: bfloat16 [4, 1024, 4096], P('dp', 'ctx'), may hold values from -6 to 6
- short_weights: float32 [3, 3, 4096], replicated, may hold values from -3.5 to 3.5
- filters: bfloat16 [512, 256], replicated, may hold values from -0.25 to 0.25
- reach_panels: int32 [256], replicated, may hold values from 1 to 4, as said below
- cotangent: bfloat16 [4, 1024, 4096], P('dp', 'ctx'), may hold values from -6 to 6
Outputs:
- layer_out: bfloat16 [4, 1024, 4096], P('dp', 'ctx')
- input_grad: bfloat16 [4, 1024, 4096], P('dp', 'ctx')
- filter_grad: float32 [512, 256], replicated
- short_grad: float32 [3, 3, 4096], replicated
The draws below stay inside these ranges and needn't reach their ends.
Inputs may be any that keep to these rules, and one draw needn't show every extreme that they name: `reach_panels`: each group's reach counts panels of 128 positions; some group reaches 4.
All inputs are finite; a program needn't handle non-finite values.
Results may differ from the reference program's by a relative error of at most 0.0051.
Values may be sent and summed in bfloat16 or wider, within the bound.
A program may use at most 128 MiB of HBM per device.

```python
import jax
import jax.numpy as jnp
from jax import lax

C = 4096
GROUPS = 256
PANEL = 128
RMAX = 4
FILTER_LEN = 512
TOKENS = 1024
SEQS = 4


def draw_reach_panels(key, part):
    first, second = jax.random.split(jax.random.fold_in(key, 11))
    values = jax.random.randint(first, (GROUPS,), 1, RMAX + 1)
    chosen = jax.random.randint(second, (), 0, GROUPS)
    return jnp.where(jnp.arange(GROUPS) == chosen, RMAX, values).astype(jnp.int32)


def steps_of(stream_key, shape, shards, least, high):
    def one(dim, shards_of):
        steps = jax.random.uniform(jax.random.fold_in(jax.random.fold_in(stream_key, 6), dim), (shards_of,), jnp.float32, least / len(shards), high / len(shards))
        return jnp.repeat(jnp.exp(steps), shape[dim] // shards_of).reshape((-1,) + (1,) * (len(shape) - dim - 1))

    level = one(*shards[0])
    for cut in shards[1:]:
        level = level * one(*cut)
    return level


def centred(own_key, dims, deviation, most, cuts=(), kind=jnp.bfloat16):
    level = steps_of(own_key, dims, cuts, -0.22, 0.18) if cuts else 1.0
    values = jax.random.normal(own_key, dims, jnp.float32) * deviation * level
    return jnp.minimum(jnp.maximum(values, -most), most).astype(kind)


def setup_inputs(seed: int = 0) -> dict:
    seeds = jax.random.split(jax.random.key(seed), 6)
    return {
        "features": centred(seeds[0], (SEQS, TOKENS, C), 1.0, 6.0, ((0, 4), (1, 8))),
        "short_weights": centred(seeds[1], (3, 3, C), 3 ** -0.5, 3.5, (), jnp.float32),
        "filters": centred(seeds[2], (FILTER_LEN, GROUPS), FILTER_LEN ** -0.5, 0.25),
        "reach_panels": draw_reach_panels(jax.random.fold_in(seeds[5], 71), 0),
        "cotangent": centred(seeds[4], (SEQS, TOKENS, C), 1.0, 6.0, ((0, 4), (1, 8))),
    }


def short_conv(extended, tap_weights):
    length = extended.shape[1] - 2
    return (tap_weights[0] * extended[:, 2:, :] + tap_weights[1] * extended[:, 1:length + 1, :]
            + tap_weights[2] * extended[:, :length, :])


def toeplitz_block(masked_t, offset, panel_rows):
    filter_len = masked_t.shape[1]
    lag_index = (offset * panel_rows + lax.broadcasted_iota(jnp.int32, (panel_rows, panel_rows), 0)
                 - lax.broadcasted_iota(jnp.int32, (panel_rows, panel_rows), 1))
    inside = (lag_index >= 0) & (lag_index < filter_len)
    picked = jnp.take(masked_t, jnp.clip(lag_index, 0, filter_len - 1), axis=1)
    return jnp.where(inside[None, :, :], picked, jnp.zeros((), masked_t.dtype))


def lag_sums(blocks):
    groups, panel_rows = blocks.shape[0], blocks.shape[1]
    flipped = blocks[:, :, ::-1]
    padded = jnp.pad(flipped, ((0, 0), (0, 0), (0, panel_rows)))
    flattened = padded.reshape(groups, 2 * panel_rows * panel_rows)[:, :panel_rows * (2 * panel_rows - 1)]
    return jnp.sum(flattened.reshape(groups, panel_rows, 2 * panel_rows - 1), axis=1)


def reference(features, short_weights, filters, reach_panels, cotangent):
    filter_len, groups = filters.shape
    length, channels = features.shape[1], features.shape[2]
    panels = length // PANEL
    lag_pos = lax.broadcasted_iota(jnp.int32, (filter_len, groups), 0)
    keep = lag_pos < reach_panels[None, :] * PANEL
    masked = jnp.where(keep, filters, jnp.zeros((), filters.dtype))
    masked_t = masked.T
    toeplitz_all = [toeplitz_block(masked_t, offset, PANEL).astype(jnp.float32) for offset in range(RMAX)]

    def one_sequence(carry, inputs):
        accum, short_acc = carry
        seq_feat, seq_cot = inputs
        extended = jnp.pad(seq_feat.astype(jnp.float32)[None], ((0, 0), (2, 0), (0, 0)))
        queries = short_conv(extended, short_weights[0])[0]
        key_feat = short_conv(extended, short_weights[1])[0]
        value_feat = short_conv(extended, short_weights[2])[0]
        mixed = (key_feat * value_feat).astype(jnp.bfloat16)
        cot_float = seq_cot.astype(jnp.float32)
        grad_conv = (cot_float * queries).astype(jnp.bfloat16)
        mixed_split = mixed.astype(jnp.float32).reshape(panels, PANEL, groups, 16)
        grad_split = grad_conv.astype(jnp.float32).reshape(panels, PANEL, groups, 16)
        total = jnp.zeros(mixed_split.shape, jnp.float32)
        back = jnp.zeros(mixed_split.shape, jnp.float32)
        for offset in range(RMAX):
            earlier = jnp.pad(mixed_split, ((offset, 0), (0, 0), (0, 0), (0, 0)))[:panels]
            later = jnp.pad(grad_split, ((0, offset), (0, 0), (0, 0), (0, 0)))[offset:]
            total = total + jnp.einsum('gts,nsgc->ntgc', toeplitz_all[offset], earlier)
            back = back + jnp.einsum('gts,ntgc->nsgc', toeplitz_all[offset], later)
            products = jnp.einsum('ntgc,nsgc->gts', grad_split, earlier)
            accum = accum.at[:, offset * PANEL + 1:offset * PANEL + 2 * PANEL].add(lag_sums(products))
        conv_out = total.reshape(length, channels)
        out_seq = (queries * conv_out).astype(jnp.bfloat16)
        grad_query = cot_float * conv_out
        grad_mixed = back.reshape(length, channels)
        stacked = jnp.stack([grad_query, grad_mixed * value_feat, grad_mixed * key_feat])
        after = jnp.pad(stacked, ((0, 0), (0, 2), (0, 0)))
        grad_in = jnp.zeros((length, channels), jnp.float32)
        for stream in range(3):
            for tap in range(3):
                grad_in = grad_in + short_weights[stream, tap] * after[stream, tap:tap + length]
        short_part = jnp.stack([jnp.stack([jnp.sum(stacked[stream] * extended[0, 2 - tap:2 - tap + length], axis=0)
                                           for tap in range(3)]) for stream in range(3)])
        return (accum, short_acc + short_part), (out_seq, grad_in.astype(jnp.bfloat16))

    start = (jnp.zeros((groups, filter_len + 2 * PANEL), jnp.float32), jnp.zeros((3, 3, channels), jnp.float32))
    (accum, short_grad), (layer_out, input_grad) = lax.scan(one_sequence, start, (features, cotangent))
    filter_grad = jnp.where(keep, accum[:, PANEL:PANEL + filter_len].T, jnp.zeros((), jnp.float32))
    return layer_out, input_grad, filter_grad, short_grad
```

```python
import functools

import jax
import jax.numpy as jnp
from jax import lax
from jax.experimental import pallas as pl
from jax.experimental.pallas import tpu as pltpu
from jax.sharding import PartitionSpec as P

PANEL = 128
UNIT = 16
TILE = 128
TAPS = 3


def rows_down(x, rows):
    return jnp.concatenate([jnp.zeros((rows, x.shape[1]), x.dtype), x[:-rows]], axis=0)


def rows_up(x, rows):
    return jnp.concatenate([x[rows:], jnp.zeros((rows, x.shape[1]), x.dtype)], axis=0)


def toeplitz(taps):
    width = taps.shape[1]
    x = jnp.broadcast_to(taps, (8, width))
    row = lax.broadcasted_iota(jnp.int32, (8, width), 0)
    for bit in (1, 2, 4):
        x = jnp.where((row & bit) != 0, pltpu.roll(x, bit, 1), x)
    rows = 8
    while rows < PANEL:
        x = jnp.concatenate([x, pltpu.roll(x, rows, 1)], axis=0)
        rows *= 2
    return x


def causal():
    shape = (PANEL, PANEL)
    return lax.broadcasted_iota(jnp.int32, shape, 1) >= lax.broadcasted_iota(jnp.int32, shape, 0)


def lag_sums(products):
    width = products.shape[1]
    first = jnp.where(causal(), products[:, :PANEL], 0.0)
    x = jnp.concatenate([first, products[:, PANEL:]], axis=1)
    rows = PANEL // 2
    while rows >= 8:
        x = x[:rows] + pltpu.roll(x[rows:], width - rows, 1)
        rows //= 2
    for step in (4, 2, 1):
        x = x + pltpu.roll(pltpu.roll(x, 8 - step, 0), width - step, 1)
    return x[0:1]


def tile_terms(reach, panels, ft, ct, wt, taps, mixed_ext, grads_ext, out_t, in_t, fg, sg_t):
    rows = panels * UNIT
    pad = (reach - 1) * UNIT
    mixed_ext[0:pad, :] = jnp.zeros((pad, PANEL), jnp.bfloat16)
    grads_ext[rows : rows + pad, :] = jnp.zeros((pad, PANEL), jnp.bfloat16)

    def group(g, carry):
        first = pl.multiple_of(g * UNIT, UNIT)
        lane = lax.broadcasted_iota(jnp.int32, (rows, PANEL), 1)
        chan = pl.ds(first, UNIT)
        feat = ft[:, chan, :].reshape(rows, PANEL)
        cot = ct[:, chan, :].reshape(rows, PANEL)
        w_all = wt[chan, :]

        def weigh(k, x):
            w = jnp.broadcast_to(w_all[:, k : k + 1], (UNIT, PANEL))
            return (x.reshape(panels, UNIT, PANEL) * w[None]).reshape(rows, PANEL)

        feats = [feat]
        for tap in range(1, TAPS):
            turned = pltpu.roll(feat, tap, 1)
            feats.append(jnp.where(lane < tap, rows_down(turned, UNIT), turned))
        streams = []
        for m in range(3):
            total = weigh(m * TAPS, feats[0])
            for tap in range(1, TAPS):
                total = total + weigh(m * TAPS + tap, feats[tap])
            streams.append(total)
        query, key, value = streams
        mixed = (key * value).astype(jnp.bfloat16)
        grad_conv = (cot * query).astype(jnp.bfloat16)
        mixed_ext[pad : pad + rows, :] = mixed
        grads_ext[0:rows, :] = grad_conv
        earlier = jnp.concatenate(
            [mixed_ext[pad - o * UNIT : pad - o * UNIT + rows, :] for o in range(reach)], axis=1
        )
        later = jnp.concatenate(
            [grads_ext[o * UNIT : o * UNIT + rows, :] for o in range(reach)], axis=1
        )
        spread = toeplitz(taps[pl.ds(g, 1), :])
        spread = jnp.concatenate(
            [jnp.where(causal(), spread[:, :PANEL], 0.0), spread[:, PANEL:]], axis=1
        ).astype(jnp.bfloat16)
        stacked = jnp.concatenate(
            [spread[:, o * PANEL : (o + 1) * PANEL] for o in range(reach)], axis=0
        )
        conv = jnp.dot(earlier, stacked, preferred_element_type=jnp.float32)
        back = lax.dot_general(
            later, spread, (((1,), (1,)), ((), ())), preferred_element_type=jnp.float32
        )
        products = lax.dot_general(
            mixed, later, (((0,), (0,)), ((), ())), preferred_element_type=jnp.float32
        )
        fg[pl.ds(g, 1), :] = lag_sums(products)
        out_t[:, chan, :] = (query * conv).reshape(panels, UNIT, PANEL)
        grads = (cot * conv, back * value, back * key)
        grad_in = None
        for tap in range(TAPS):
            part = weigh(tap, grads[0]) + weigh(TAPS + tap, grads[1]) + weigh(2 * TAPS + tap, grads[2])
            if tap:
                turned = pltpu.roll(part, PANEL - tap, 1)
                part = jnp.where(lane >= PANEL - tap, rows_up(turned, UNIT), turned)
            grad_in = part if grad_in is None else grad_in + part
        in_t[:, chan, :] = grad_in.reshape(panels, UNIT, PANEL)
        small_lane = lax.broadcasted_iota(jnp.int32, (UNIT, PANEL), 1)
        sums = jnp.zeros((UNIT, PANEL), jnp.float32)
        for m in range(3):
            for tap in range(TAPS):
                part = jnp.sum((grads[m] * feats[tap]).reshape(panels, UNIT, PANEL), axis=0)
                sums = jnp.where(small_lane == m * TAPS + tap, jnp.sum(part, axis=1, keepdims=True), sums)
        sg_t[chan, :] = sums
        return carry

    lax.fori_loop(0, TILE // UNIT, group, 0)


def local_kernel(reach, panels, f_ref, c_ref, wt, taps, out_ref, in_ref, fg, sg, ft, ct, out_t, in_t, sg_t, mixed_ext, grads_ext):
    def turn_in(n, carry):
        rows = pl.ds(pl.multiple_of(n * PANEL, PANEL), PANEL)
        ft[n] = f_ref[rows, :].astype(jnp.float32).T
        ct[n] = c_ref[rows, :].astype(jnp.float32).T
        return carry

    lax.fori_loop(0, panels, turn_in, 0)
    tile_terms(reach, panels, ft, ct, wt, taps, mixed_ext, grads_ext, out_t, in_t, fg, sg_t)
    sg[...] = sg_t[...].T[:UNIT]

    def turn_out(n, carry):
        rows = pl.ds(pl.multiple_of(n * PANEL, PANEL), PANEL)
        out_ref[rows, :] = out_t[n].T.astype(jnp.bfloat16)
        in_ref[rows, :] = in_t[n].T.astype(jnp.bfloat16)
        return carry

    lax.fori_loop(0, panels, turn_out, 0)


def shards(features, short_weights, filters, reach_panels, cotangent):
    filter_len, groups = filters.shape
    channels = features.shape[2]
    reach = filter_len // PANEL
    lag_pos = lax.broadcasted_iota(jnp.int32, (filter_len, groups), 0)
    keep = lag_pos < reach_panels[None, :] * PANEL
    masked = jnp.where(keep, filters, jnp.zeros((), filters.dtype))
    f_all = lax.all_to_all(features[0], "ctx", split_axis=1, concat_axis=0, tiled=True)
    c_all = lax.all_to_all(cotangent[0], "ctx", split_axis=1, concat_axis=0, tiled=True)
    length, width = f_all.shape
    panels = length // PANEL
    me = lax.axis_index("ctx")
    units = width // UNIT
    taps = lax.dynamic_slice_in_dim(masked, me * units, units, 1).T.astype(jnp.float32)
    wt = lax.dynamic_slice_in_dim(short_weights.reshape(9, channels), me * width, width, 1).T
    tile_units = TILE // UNIT
    big = lambda: pl.BlockSpec((length, TILE), lambda j: (0, j))
    out_local, in_local, fg, sg = pl.pallas_call(
        functools.partial(local_kernel, reach, panels),
        grid=(width // TILE,),
        in_specs=[
            big(),
            big(),
            pl.BlockSpec((TILE, 9), lambda j: (j, 0)),
            pl.BlockSpec((tile_units, filter_len), lambda j: (j, 0)),
        ],
        out_specs=[
            big(),
            big(),
            pl.BlockSpec((tile_units, filter_len), lambda j: (j, 0)),
            pl.BlockSpec((UNIT, TILE), lambda j: (0, j)),
        ],
        out_shape=[
            jax.ShapeDtypeStruct((length, width), jnp.bfloat16),
            jax.ShapeDtypeStruct((length, width), jnp.bfloat16),
            jax.ShapeDtypeStruct((units, filter_len), jnp.float32),
            jax.ShapeDtypeStruct((UNIT, width), jnp.float32),
        ],
        scratch_shapes=[pltpu.VMEM((panels, TILE, PANEL), jnp.float32)] * 4
        + [
            pltpu.VMEM((TILE, PANEL), jnp.float32),
            pltpu.VMEM(((panels + reach - 1) * UNIT, PANEL), jnp.bfloat16),
            pltpu.VMEM(((panels + reach - 1) * UNIT, PANEL), jnp.bfloat16),
        ],
        compiler_params=pltpu.CompilerParams(vmem_limit_bytes=40 * 2**20),
    )(f_all, c_all, wt, taps)
    layer_out = lax.all_to_all(out_local, "ctx", split_axis=0, concat_axis=1, tiled=True)[None]
    input_grad = lax.all_to_all(in_local, "ctx", split_axis=0, concat_axis=1, tiled=True)[None]
    flat = jnp.concatenate([fg.reshape(-1), sg[:9].reshape(-1)])
    flat = lax.psum(flat, "dp")
    every = lax.all_gather(flat, "ctx")
    cut = units * filter_len
    filter_sum = every[:, :cut].reshape(groups, filter_len).T
    filter_grad = jnp.where(keep, filter_sum, jnp.zeros((), jnp.float32))
    short_grad = every[:, cut:].reshape(-1, 9, width).transpose(1, 0, 2).reshape(3, 3, channels)
    return (layer_out, input_grad, filter_grad, short_grad)


def solution(mesh):
    return jax.shard_map(
        shards,
        mesh=mesh,
        in_specs=(P("dp", "ctx", None), P(), P(), P(), P("dp", "ctx", None)),
        out_specs=(P("dp", "ctx", None), P("dp", "ctx", None), P(), P()),
        check_vma=False,
    )
```

```python
import functools

import jax
import jax.numpy as jnp
from jax import lax
from jax.experimental import pallas as pl
from jax.experimental.pallas import tpu as pltpu
from jax.sharding import PartitionSpec as P

PANEL = 128
UNIT = 16
TILE = 128
TAPS = 3
UNROLL = 2
MESH = pl.DeviceIdType.MESH


def rows_down(x, rows):
    return jnp.concatenate([jnp.zeros((rows, x.shape[1]), x.dtype), x[:-rows]], axis=0)


def rows_up(x, rows):
    return jnp.concatenate([x[rows:], jnp.zeros((rows, x.shape[1]), x.dtype)], axis=0)


def toeplitz(taps):
    width = taps.shape[1]
    x = jnp.broadcast_to(taps, (8, width))
    row = lax.broadcasted_iota(jnp.int32, (8, width), 0)
    for bit in (1, 2, 4):
        x = jnp.where((row & bit) != 0, pltpu.roll(x, bit, 1), x)
    rows = 8
    while rows < PANEL:
        x = jnp.concatenate([x, pltpu.roll(x, rows, 1)], axis=0)
        rows *= 2
    return x


def causal():
    shape = (PANEL, PANEL)
    return lax.broadcasted_iota(jnp.int32, shape, 1) >= lax.broadcasted_iota(jnp.int32, shape, 0)


def lag_sums(products):
    width = products.shape[1]
    first = jnp.where(causal(), products[:, :PANEL], 0.0)
    x = jnp.concatenate([first, products[:, PANEL:]], axis=1)
    rows = PANEL // 2
    while rows >= 8:
        x = x[:rows] + pltpu.roll(x[rows:], width - rows, 1)
        rows //= 2
    for step in (4, 2, 1):
        x = x + pltpu.roll(pltpu.roll(x, 8 - step, 0), width - step, 1)
    return x[0:1]


def tile_terms(reach, panels, ft, ct, wt, taps, out_t, in_t, fg, sg_t):
    rows = panels * UNIT

    def group(g, carry):
        first = pl.multiple_of(g * UNIT, UNIT)
        lane = lax.broadcasted_iota(jnp.int32, (rows, PANEL), 1)
        chan = pl.ds(first, UNIT)
        feat = ft[:, chan, :].reshape(rows, PANEL)
        cot = ct[:, chan, :].reshape(rows, PANEL)
        w_all = wt[chan, :]

        def weigh(k, x):
            w = jnp.broadcast_to(w_all[:, k : k + 1], (UNIT, PANEL))
            return (x.reshape(panels, UNIT, PANEL) * w[None]).reshape(rows, PANEL)

        feats = [feat]
        for tap in range(1, TAPS):
            turned = pltpu.roll(feat, tap, 1)
            feats.append(jnp.where(lane < tap, rows_down(turned, UNIT), turned))
        streams = []
        for m in range(3):
            total = weigh(m * TAPS, feats[0])
            for tap in range(1, TAPS):
                total = total + weigh(m * TAPS + tap, feats[tap])
            streams.append(total)
        query, key, value = streams
        mixed = (key * value).astype(jnp.bfloat16)
        grad_conv = (cot * query).astype(jnp.bfloat16)
        earlier = jnp.concatenate(
            [mixed] + [rows_down(mixed, o * UNIT) for o in range(1, reach)], axis=1
        )
        later = jnp.concatenate(
            [grad_conv] + [rows_up(grad_conv, o * UNIT) for o in range(1, reach)], axis=1
        )
        spread = toeplitz(taps[pl.ds(g, 1), :])
        spread = jnp.concatenate(
            [jnp.where(causal(), spread[:, :PANEL], 0.0), spread[:, PANEL:]], axis=1
        ).astype(jnp.bfloat16)
        stacked = jnp.concatenate(
            [spread[:, o * PANEL : (o + 1) * PANEL] for o in range(reach)], axis=0
        )
        conv = jnp.dot(earlier, stacked, preferred_element_type=jnp.float32)
        back = lax.dot_general(
            later, spread, (((1,), (1,)), ((), ())), preferred_element_type=jnp.float32
        )
        products = lax.dot_general(
            mixed, later, (((0,), (0,)), ((), ())), preferred_element_type=jnp.float32
        )
        fg[pl.ds(g, 1), :] = lag_sums(products)
        out_t[:, chan, :] = (query * conv).reshape(panels, UNIT, PANEL)
        grads = (cot * conv, back * value, back * key)
        grad_in = None
        for tap in range(TAPS):
            part = weigh(tap, grads[0]) + weigh(TAPS + tap, grads[1]) + weigh(2 * TAPS + tap, grads[2])
            if tap:
                turned = pltpu.roll(part, PANEL - tap, 1)
                part = jnp.where(lane >= PANEL - tap, rows_up(turned, UNIT), turned)
            grad_in = part if grad_in is None else grad_in + part
        in_t[:, chan, :] = grad_in.reshape(panels, UNIT, PANEL)
        small_lane = lax.broadcasted_iota(jnp.int32, (UNIT, PANEL), 1)
        sums = jnp.zeros((UNIT, PANEL), jnp.float32)
        for m in range(3):
            for tap in range(TAPS):
                part = jnp.sum((grads[m] * feats[tap]).reshape(panels, UNIT, PANEL), axis=0)
                sums = jnp.where(small_lane == m * TAPS + tap, jnp.sum(part, axis=1, keepdims=True), sums)
        sg_t[chan, :] = sums
        return carry

    lax.fori_loop(0, TILE // UNIT, group, 0, unroll=UNROLL)


def layer_kernel(
    reach, ndp, nctx, f_hbm, c_hbm, wt, taps, out_hbm, in_hbm, all_hbm,
    arrived, leaving, ft, ct, out_t, in_t, fg, sg_t, pay, parts, sums,
    own_sem, in_send, in_recv, out_send, out_recv, keep_sem,
    rs_send, rs_recv, gd_send, gd_recv, gd_own, gc_send, gc_recv,
):
    dp, me = lax.axis_index("dp"), lax.axis_index("ctx")
    width = arrived.shape[3]
    tiles = width // TILE
    chunk = sums.shape[1]
    ins, outs = (f_hbm, c_hbm), (out_hbm, in_hbm)

    def ctx_peer(k):
        return lax.rem(me + k, nctx)

    def dp_peer(k):
        return lax.rem(dp + k, ndp)

    def lanes(j):
        return pl.ds(pl.multiple_of(j * TILE, TILE), TILE)

    def cols(owner, j):
        return pl.ds(pl.multiple_of(owner * width + j * TILE, TILE), TILE)

    def copy(src, dst, send, recv, device):
        return pltpu.make_async_remote_copy(
            src_ref=src, dst_ref=dst, send_sem=send, recv_sem=recv, device_id=device, device_id_type=MESH
        )

    def in_copy(a, j, k, slot):
        return copy(
            ins[a].at[:, cols(ctx_peer(k), j)],
            arrived.at[a, slot, :, lanes(j)],
            in_send.at[a, j, k],
            in_recv.at[a, j, k],
            (dp, ctx_peer(k)),
        )

    def in_own(a, j):
        return pltpu.make_async_copy(
            ins[a].at[:, cols(me, j)], arrived.at[a, me, :, lanes(j)], own_sem.at[a, j]
        )

    def out_copy(a, j, k, slot):
        return copy(
            leaving.at[a, ctx_peer(k), :, lanes(j)],
            outs[a].at[:, cols(slot, j)],
            out_send.at[a, j, k],
            out_recv.at[a, j, k],
            (dp, ctx_peer(k)),
        )

    def out_own(a, j):
        return pltpu.make_async_copy(
            leaving.at[a, me, :, lanes(j)], outs[a].at[:, cols(me, j)], keep_sem.at[a, j]
        )

    def rs_copy(j, k):
        return copy(
            pay.at[j, dp_peer(k)], parts.at[j, k], rs_send.at[j, k], rs_recv.at[j, k], (dp_peer(k), me)
        )

    def gd_copy(j, k, slot):
        return copy(
            sums.at[j], all_hbm.at[me, j, slot], gd_send.at[j, k], gd_recv.at[j, k], (dp_peer(k), me)
        )

    def gd_keep(j):
        return pltpu.make_async_copy(sums.at[j], all_hbm.at[me, j, dp], gd_own.at[j])

    def gc_copy(j, k, slot):
        return copy(
            all_hbm.at[me, j], all_hbm.at[slot, j], gc_send.at[j, k], gc_recv.at[j, k], (dp, ctx_peer(k))
        )

    def each(count, body):
        def step(i, carry):
            body(i)
            return carry

        lax.fori_loop(0, count, step, 0)

    barrier = pltpu.get_barrier_semaphore()
    for k in range(1, nctx):
        pl.semaphore_signal(barrier, inc=1, device_id=(dp, ctx_peer(k)), device_id_type=MESH)
    for k in range(1, ndp):
        pl.semaphore_signal(barrier, inc=1, device_id=(dp_peer(k), me), device_id_type=MESH)
    for a in range(2):
        each(tiles, lambda j: in_own(a, j).start())
    pl.semaphore_wait(barrier, nctx + ndp - 2)

    def send_in(j):
        for a in range(2):
            each(nctx - 1, lambda i: in_copy(a, j, i + 1, me).start())

    each(tiles, send_in)

    def spread_dp(j):
        each(ndp - 1, lambda i: rs_copy(j, i + 1).wait_recv())
        total = pay[j, dp]
        for k in range(1, ndp):
            total = total + parts[j, k]
        sums[j] = total
        gd_keep(j).start()
        each(ndp - 1, lambda i: gd_copy(j, i + 1, dp).start())

    def spread_ctx(j):
        gd_keep(j).wait()
        each(ndp - 1, lambda i: gd_copy(j, i + 1, lax.rem(dp + ndp - i - 1, ndp)).wait_recv())
        each(nctx - 1, lambda i: gc_copy(j, i + 1, me).start())

    def one_tile(j):
        for a in range(2):
            in_own(a, j).wait()
            each(
                nctx - 1,
                lambda i: in_copy(a, j, i + 1, lax.rem(me + nctx - i - 1, nctx)).wait_recv(),
            )

        def turn_in(n):
            ft[n] = arrived[0, n, :, lanes(j)].astype(jnp.float32).T
            ct[n] = arrived[1, n, :, lanes(j)].astype(jnp.float32).T

        each(nctx, turn_in)
        units = TILE // UNIT
        tile_terms(
            reach, nctx, ft, ct, wt.at[lanes(j), :],
            taps.at[pl.ds(pl.multiple_of(j * units, units), units), :], out_t, in_t, fg, sg_t,
        )

        def turn_out(n):
            leaving[0, n, :, lanes(j)] = out_t[n].T.astype(jnp.bfloat16)
            leaving[1, n, :, lanes(j)] = in_t[n].T.astype(jnp.bfloat16)

        each(nctx, turn_out)
        rows = [fg[:, o * PANEL : (o + 1) * PANEL] for o in range(reach)] + [sg_t[...].T[:UNIT]]
        filled = reach * units + UNIT
        if filled < ndp * chunk:
            rows.append(jnp.zeros((ndp * chunk - filled, PANEL), jnp.float32))
        pay[j] = jnp.concatenate(rows, axis=0).reshape(ndp, chunk, PANEL)
        each(ndp - 1, lambda i: rs_copy(j, i + 1).start())
        for a in range(2):
            out_own(a, j).start()
            each(nctx - 1, lambda i: out_copy(a, j, i + 1, me).start())

        @pl.when(j >= 1)
        def _():
            spread_dp(j - 1)

        @pl.when(j >= 2)
        def _():
            spread_ctx(j - 2)

    each(tiles, one_tile)
    if tiles >= 2:
        spread_ctx(tiles - 2)
    spread_dp(tiles - 1)
    spread_ctx(tiles - 1)

    def finish(j):
        for a in range(2):
            each(nctx - 1, lambda i: in_copy(a, j, i + 1, me).wait_send())
            out_own(a, j).wait()
            each(nctx - 1, lambda i: out_copy(a, j, i + 1, me).wait_send())
            each(
                nctx - 1,
                lambda i: out_copy(a, j, i + 1, lax.rem(me + nctx - i - 1, nctx)).wait_recv(),
            )
        each(ndp - 1, lambda i: rs_copy(j, i + 1).wait_send())
        each(ndp - 1, lambda i: gd_copy(j, i + 1, dp).wait_send())
        each(nctx - 1, lambda i: gc_copy(j, i + 1, me).wait_send())
        each(nctx - 1, lambda i: gc_copy(j, i + 1, lax.rem(me + nctx - i - 1, nctx)).wait_recv())

    each(tiles, finish)


def shards(ndp, nctx, features, short_weights, filters, reach_panels, cotangent):
    filter_len, groups = filters.shape
    channels = features.shape[2]
    reach = filter_len // PANEL
    lag_pos = lax.broadcasted_iota(jnp.int32, (filter_len, groups), 0)
    keep = lag_pos < reach_panels[None, :] * PANEL
    masked = jnp.where(keep, filters, jnp.zeros((), filters.dtype))
    rows = features.shape[1]
    assert rows == PANEL and features.shape[0] == 1
    width = channels // nctx
    tiles = width // TILE
    me = lax.axis_index("ctx")
    units = width // UNIT
    tile_units = TILE // UNIT
    taps = lax.dynamic_slice_in_dim(masked, me * units, units, 1).T.astype(jnp.float32)
    wt = lax.dynamic_slice_in_dim(short_weights.reshape(9, channels), me * width, width, 1).T
    filled = reach * tile_units + UNIT
    chunk = -(-filled // (8 * ndp)) * 8
    hbm = pl.BlockSpec(memory_space=pl.ANY)
    vmem = pl.BlockSpec(memory_space=pltpu.VMEM)
    dma = pltpu.SemaphoreType.DMA
    turned = pltpu.VMEM((nctx, TILE, PANEL), jnp.float32)
    layer_out, input_grad, every = pl.pallas_call(
        functools.partial(layer_kernel, reach, ndp, nctx),
        in_specs=[hbm, hbm, vmem, vmem],
        out_specs=[hbm, hbm, hbm],
        out_shape=[
            jax.ShapeDtypeStruct((rows, channels), jnp.bfloat16),
            jax.ShapeDtypeStruct((rows, channels), jnp.bfloat16),
            jax.ShapeDtypeStruct((nctx, tiles, ndp, chunk, PANEL), jnp.float32),
        ],
        scratch_shapes=[
            pltpu.VMEM((2, nctx, PANEL, width), jnp.bfloat16),
            pltpu.VMEM((2, nctx, PANEL, width), jnp.bfloat16),
            turned,
            turned,
            turned,
            turned,
            pltpu.VMEM((tile_units, filter_len), jnp.float32),
            pltpu.VMEM((TILE, PANEL), jnp.float32),
            pltpu.VMEM((tiles, ndp, chunk, PANEL), jnp.float32),
            pltpu.VMEM((tiles, ndp, chunk, PANEL), jnp.float32),
            pltpu.VMEM((tiles, chunk, PANEL), jnp.float32),
            dma((2, tiles)),
            dma((2, tiles, nctx)),
            dma((2, tiles, nctx)),
            dma((2, tiles, nctx)),
            dma((2, tiles, nctx)),
            dma((2, tiles)),
            dma((tiles, ndp)),
            dma((tiles, ndp)),
            dma((tiles, ndp)),
            dma((tiles, ndp)),
            dma((tiles,)),
            dma((tiles, nctx)),
            dma((tiles, nctx)),
        ],
        compiler_params=pltpu.CompilerParams(
            collective_id=0, has_side_effects=True, vmem_limit_bytes=48 * 2**20
        ),
    )(features[0], cotangent[0], wt, taps)
    every = every.reshape(nctx, tiles, ndp * chunk, PANEL)
    lag_rows = every[:, :, : reach * tile_units].reshape(nctx, tiles, reach, tile_units, PANEL)
    filter_sum = lag_rows.transpose(2, 4, 0, 1, 3).reshape(filter_len, groups)
    filter_grad = jnp.where(keep, filter_sum, jnp.zeros((), jnp.float32))
    short_rows = every[:, :, reach * tile_units : reach * tile_units + 9]
    short_grad = short_rows.transpose(2, 0, 1, 3).reshape(3, 3, channels)
    return (layer_out[None], input_grad[None], filter_grad, short_grad)


def solution(mesh):
    return jax.shard_map(
        functools.partial(shards, mesh.shape["dp"], mesh.shape["ctx"]),
        mesh=mesh,
        in_specs=(P("dp", "ctx", None), P(), P(), P(), P("dp", "ctx", None)),
        out_specs=(P("dp", "ctx", None), P("dp", "ctx", None), P(), P()),
        check_vma=False,
    )
```

```python
import functools

import jax
import jax.numpy as jnp
from jax import lax
from jax.experimental import pallas as pl
from jax.experimental.pallas import tpu as pltpu
from jax.sharding import PartitionSpec as P

PANEL = 128
UNIT = 16
TILE = 128
TAPS = 3
UNROLL = 4
MESH = pl.DeviceIdType.MESH


def rows_down(x, rows):
    return jnp.concatenate([jnp.zeros((rows, x.shape[1]), x.dtype), x[:-rows]], axis=0)


def rows_up(x, rows):
    return jnp.concatenate([x[rows:], jnp.zeros((rows, x.shape[1]), x.dtype)], axis=0)


def causal():
    shape = (PANEL, PANEL)
    return lax.broadcasted_iota(jnp.int32, shape, 1) >= lax.broadcasted_iota(jnp.int32, shape, 0)


def toeplitz(taps):
    width = taps.shape[1]
    x = jnp.broadcast_to(taps, (8, width))
    row = lax.broadcasted_iota(jnp.int32, (8, width), 0)
    for bit in (1, 2, 4):
        x = jnp.where((row & bit) != 0, pltpu.roll(x, bit, 1), x)
    rows = 8
    while rows < PANEL:
        x = jnp.concatenate([x, pltpu.roll(x, rows, 1)], axis=0)
        rows *= 2
    first = jnp.where(causal(), x[:, :PANEL], 0.0)
    return jnp.concatenate([first, x[:, PANEL:]], axis=1).astype(jnp.bfloat16)


def lag_sums(products):
    width = products.shape[1]
    first = jnp.where(causal(), products[:, :PANEL], 0.0)
    x = jnp.concatenate([first, products[:, PANEL:]], axis=1)
    rows = PANEL // 2
    while rows >= 8:
        x = x[:rows] + pltpu.roll(x[rows:], width - rows, 1)
        rows //= 2
    for step in (4, 2, 1):
        x = x + pltpu.roll(pltpu.roll(x, 8 - step, 0), width - step, 1)
    return x[0:1]


def tile_terms(reach, panels, ft, ct, wt, spreads, out_t, in_t, fg, sg_t):
    rows = panels * UNIT

    def group(g, carry):
        first = pl.multiple_of(g * UNIT, UNIT)
        lane = lax.broadcasted_iota(jnp.int32, (rows, PANEL), 1)
        chan = pl.ds(first, UNIT)
        feat = ft[:, chan, :].reshape(rows, PANEL)
        cot = ct[:, chan, :].reshape(rows, PANEL)
        w_all = wt[chan, :]

        def weigh(k, x):
            w = jnp.broadcast_to(w_all[:, k : k + 1], (UNIT, PANEL))
            return (x.reshape(panels, UNIT, PANEL) * w[None]).reshape(rows, PANEL)

        feats = [feat]
        for tap in range(1, TAPS):
            turned = pltpu.roll(feat, tap, 1)
            feats.append(jnp.where(lane < tap, rows_down(turned, UNIT), turned))
        streams = []
        for m in range(3):
            total = weigh(m * TAPS, feats[0])
            for tap in range(1, TAPS):
                total = total + weigh(m * TAPS + tap, feats[tap])
            streams.append(total)
        query, key, value = streams
        mixed = (key * value).astype(jnp.bfloat16)
        grad_conv = (cot * query).astype(jnp.bfloat16)
        earlier = jnp.concatenate(
            [mixed] + [rows_down(mixed, o * UNIT) for o in range(1, reach)], axis=1
        )
        later = jnp.concatenate(
            [grad_conv] + [rows_up(grad_conv, o * UNIT) for o in range(1, reach)], axis=1
        )
        spread = spreads[g]
        stacked = jnp.concatenate(
            [spread[:, o * PANEL : (o + 1) * PANEL] for o in range(reach)], axis=0
        )
        conv = jnp.dot(earlier, stacked, preferred_element_type=jnp.float32)
        back = lax.dot_general(
            later, spread, (((1,), (1,)), ((), ())), preferred_element_type=jnp.float32
        )
        products = lax.dot_general(
            mixed, later, (((0,), (0,)), ((), ())), preferred_element_type=jnp.float32
        )
        fg[pl.ds(g, 1), :] = lag_sums(products)
        out_t[:, chan, :] = (query * conv).reshape(panels, UNIT, PANEL)
        grads = (cot * conv, back * value, back * key)
        grad_in = None
        for tap in range(TAPS):
            part = weigh(tap, grads[0]) + weigh(TAPS + tap, grads[1]) + weigh(2 * TAPS + tap, grads[2])
            if tap:
                turned = pltpu.roll(part, PANEL - tap, 1)
                part = jnp.where(lane >= PANEL - tap, rows_up(turned, UNIT), turned)
            grad_in = part if grad_in is None else grad_in + part
        in_t[:, chan, :] = grad_in.reshape(panels, UNIT, PANEL)
        small_lane = lax.broadcasted_iota(jnp.int32, (UNIT, PANEL), 1)
        sums = jnp.zeros((UNIT, PANEL), jnp.float32)
        for m in range(3):
            for tap in range(TAPS):
                part = jnp.sum((grads[m] * feats[tap]).reshape(panels, UNIT, PANEL), axis=0)
                sums = jnp.where(small_lane == m * TAPS + tap, jnp.sum(part, axis=1, keepdims=True), sums)
        sg_t[chan, :] = sums
        return carry

    lax.fori_loop(0, TILE // UNIT, group, 0, unroll=UNROLL)


def layer_kernel(
    reach, ndp, nctx, f_hbm, c_hbm, wt, taps, out_hbm, in_hbm, all_hbm,
    arrived, leaving, spreads, ft, ct, out_t, in_t, fg, sg_t, pay, parts, sums,
    own_sem, in_send, in_recv, out_send, out_recv, keep_sem,
    rs_send, rs_recv, gd_send, gd_recv, gd_own, gc_send, gc_recv,
):
    dp, me = lax.axis_index("dp"), lax.axis_index("ctx")
    width = arrived.shape[3]
    tiles = width // TILE
    chunk = sums.shape[1]
    ins, outs = (f_hbm, c_hbm), (out_hbm, in_hbm)

    def ctx_peer(k):
        return lax.rem(me + k, nctx)

    def dp_peer(k):
        return lax.rem(dp + k, ndp)

    def lanes(j):
        return pl.ds(pl.multiple_of(j * TILE, TILE), TILE)

    def cols(owner, j):
        return pl.ds(pl.multiple_of(owner * width + j * TILE, TILE), TILE)

    def copy(src, dst, send, recv, device):
        return pltpu.make_async_remote_copy(
            src_ref=src, dst_ref=dst, send_sem=send, recv_sem=recv, device_id=device, device_id_type=MESH
        )

    def in_copy(a, j, k, slot):
        return copy(
            ins[a].at[:, cols(ctx_peer(k), j)],
            arrived.at[a, slot, :, lanes(j)],
            in_send.at[a, j, k],
            in_recv.at[a, j, k],
            (dp, ctx_peer(k)),
        )

    def in_own(a, j):
        return pltpu.make_async_copy(
            ins[a].at[:, cols(me, j)], arrived.at[a, me, :, lanes(j)], own_sem.at[a, j]
        )

    def out_copy(a, j, k, slot):
        return copy(
            leaving.at[a, ctx_peer(k), :, lanes(j)],
            outs[a].at[:, cols(slot, j)],
            out_send.at[a, j, k],
            out_recv.at[a, j, k],
            (dp, ctx_peer(k)),
        )

    def out_own(a, j):
        return pltpu.make_async_copy(
            leaving.at[a, me, :, lanes(j)], outs[a].at[:, cols(me, j)], keep_sem.at[a, j]
        )

    def rs_copy(j, k):
        return copy(
            pay.at[j, dp_peer(k)], parts.at[j, k], rs_send.at[j, k], rs_recv.at[j, k], (dp_peer(k), me)
        )

    def gd_copy(j, k, slot):
        return copy(
            sums.at[j], all_hbm.at[me, j, slot], gd_send.at[j, k], gd_recv.at[j, k], (dp_peer(k), me)
        )

    def gd_keep(j):
        return pltpu.make_async_copy(sums.at[j], all_hbm.at[me, j, dp], gd_own.at[j])

    def gc_copy(j, k, slot):
        return copy(
            all_hbm.at[me, j], all_hbm.at[slot, j], gc_send.at[j, k], gc_recv.at[j, k], (dp, ctx_peer(k))
        )

    def each(count, body, unroll=1):
        def step(i, carry):
            body(i)
            return carry

        lax.fori_loop(0, count, step, 0, unroll=unroll)

    barrier = pltpu.get_barrier_semaphore()
    for k in range(1, nctx):
        pl.semaphore_signal(barrier, inc=1, device_id=(dp, ctx_peer(k)), device_id_type=MESH)
    for k in range(1, ndp):
        pl.semaphore_signal(barrier, inc=1, device_id=(dp_peer(k), me), device_id_type=MESH)
    for a in range(2):
        each(tiles, lambda j: in_own(a, j).start())
    pl.semaphore_wait(barrier, nctx + ndp - 2)

    def send_in(j):
        for a in range(2):
            each(nctx - 1, lambda i: in_copy(a, j, i + 1, me).start())

    each(tiles, send_in)

    def build(g):
        spreads[g] = toeplitz(taps[pl.ds(g, 1), :])

    each(taps.shape[0], build, UNROLL)

    def spread_dp(j):
        each(ndp - 1, lambda i: rs_copy(j, i + 1).wait_recv())
        total = pay[j, dp]
        for k in range(1, ndp):
            total = total + parts[j, k]
        sums[j] = total
        gd_keep(j).start()
        each(ndp - 1, lambda i: gd_copy(j, i + 1, dp).start())

    def spread_ctx(j):
        gd_keep(j).wait()
        each(ndp - 1, lambda i: gd_copy(j, i + 1, lax.rem(dp + ndp - i - 1, ndp)).wait_recv())
        each(nctx - 1, lambda i: gc_copy(j, i + 1, me).start())

    def one_tile(j):
        for a in range(2):
            in_own(a, j).wait()
            each(
                nctx - 1,
                lambda i: in_copy(a, j, i + 1, lax.rem(me + nctx - i - 1, nctx)).wait_recv(),
            )

        def turn_in(n):
            ft[n] = arrived[0, n, :, lanes(j)].astype(jnp.float32).T
            ct[n] = arrived[1, n, :, lanes(j)].astype(jnp.float32).T

        each(nctx, turn_in, UNROLL)
        units = TILE // UNIT
        tile_terms(
            reach, nctx, ft, ct, wt.at[lanes(j), :],
            spreads.at[pl.ds(j * units, units)], out_t, in_t, fg, sg_t,
        )

        def turn_out(n):
            leaving[0, n, :, lanes(j)] = out_t[n].T.astype(jnp.bfloat16)
            leaving[1, n, :, lanes(j)] = in_t[n].T.astype(jnp.bfloat16)

        each(nctx, turn_out, UNROLL)
        rows = [fg[:, o * PANEL : (o + 1) * PANEL] for o in range(reach)] + [sg_t[...].T[:UNIT]]
        filled = reach * units + UNIT
        if filled < ndp * chunk:
            rows.append(jnp.zeros((ndp * chunk - filled, PANEL), jnp.float32))
        pay[j] = jnp.concatenate(rows, axis=0).reshape(ndp, chunk, PANEL)
        each(ndp - 1, lambda i: rs_copy(j, i + 1).start())
        for a in range(2):
            out_own(a, j).start()
            each(nctx - 1, lambda i: out_copy(a, j, i + 1, me).start())

        @pl.when(j >= 1)
        def _():
            spread_dp(j - 1)

        @pl.when(j >= 2)
        def _():
            spread_ctx(j - 2)

    each(tiles, one_tile)
    if tiles >= 2:
        spread_ctx(tiles - 2)
    spread_dp(tiles - 1)
    spread_ctx(tiles - 1)

    def finish(j):
        for a in range(2):
            each(nctx - 1, lambda i: in_copy(a, j, i + 1, me).wait_send())
            out_own(a, j).wait()
            each(nctx - 1, lambda i: out_copy(a, j, i + 1, me).wait_send())
            each(
                nctx - 1,
                lambda i: out_copy(a, j, i + 1, lax.rem(me + nctx - i - 1, nctx)).wait_recv(),
            )
        each(ndp - 1, lambda i: rs_copy(j, i + 1).wait_send())
        each(ndp - 1, lambda i: gd_copy(j, i + 1, dp).wait_send())
        each(nctx - 1, lambda i: gc_copy(j, i + 1, me).wait_send())
        each(nctx - 1, lambda i: gc_copy(j, i + 1, lax.rem(me + nctx - i - 1, nctx)).wait_recv())

    each(tiles, finish)


def shards(ndp, nctx, features, short_weights, filters, reach_panels, cotangent):
    filter_len, groups = filters.shape
    channels = features.shape[2]
    reach = filter_len // PANEL
    lag_pos = lax.broadcasted_iota(jnp.int32, (filter_len, groups), 0)
    keep = lag_pos < reach_panels[None, :] * PANEL
    masked = jnp.where(keep, filters, jnp.zeros((), filters.dtype))
    rows = features.shape[1]
    assert rows == PANEL and features.shape[0] == 1
    width = channels // nctx
    tiles = width // TILE
    me = lax.axis_index("ctx")
    units = width // UNIT
    tile_units = TILE // UNIT
    taps = lax.dynamic_slice_in_dim(masked, me * units, units, 1).T.astype(jnp.float32)
    wt = lax.dynamic_slice_in_dim(short_weights.reshape(9, channels), me * width, width, 1).T
    filled = reach * tile_units + UNIT
    chunk = -(-filled // (8 * ndp)) * 8
    hbm = pl.BlockSpec(memory_space=pltpu.HBM)
    vmem = pl.BlockSpec(memory_space=pltpu.VMEM)
    dma = pltpu.SemaphoreType.DMA
    turned = pltpu.VMEM((nctx, TILE, PANEL), jnp.float32)
    layer_out, input_grad, every = pl.pallas_call(
        functools.partial(layer_kernel, reach, ndp, nctx),
        in_specs=[hbm, hbm, vmem, vmem],
        out_specs=[hbm, hbm, hbm],
        out_shape=[
            jax.ShapeDtypeStruct((rows, channels), jnp.bfloat16),
            jax.ShapeDtypeStruct((rows, channels), jnp.bfloat16),
            jax.ShapeDtypeStruct((nctx, tiles, ndp, chunk, PANEL), jnp.float32),
        ],
        scratch_shapes=[
            pltpu.VMEM((2, nctx, PANEL, width), jnp.bfloat16),
            pltpu.VMEM((2, nctx, PANEL, width), jnp.bfloat16),
            pltpu.VMEM((units, PANEL, filter_len), jnp.bfloat16),
            turned,
            turned,
            turned,
            turned,
            pltpu.VMEM((tile_units, filter_len), jnp.float32),
            pltpu.VMEM((TILE, PANEL), jnp.float32),
            pltpu.VMEM((tiles, ndp, chunk, PANEL), jnp.float32),
            pltpu.VMEM((tiles, ndp, chunk, PANEL), jnp.float32),
            pltpu.VMEM((tiles, chunk, PANEL), jnp.float32),
            dma((2, tiles)),
            dma((2, tiles, nctx)),
            dma((2, tiles, nctx)),
            dma((2, tiles, nctx)),
            dma((2, tiles, nctx)),
            dma((2, tiles)),
            dma((tiles, ndp)),
            dma((tiles, ndp)),
            dma((tiles, ndp)),
            dma((tiles, ndp)),
            dma((tiles,)),
            dma((tiles, nctx)),
            dma((tiles, nctx)),
        ],
        compiler_params=pltpu.CompilerParams(
            collective_id=0, has_side_effects=True, vmem_limit_bytes=63 * 2**20
        ),
    )(features[0], cotangent[0], wt, taps)
    every = every.reshape(nctx, tiles, ndp * chunk, PANEL)
    lag_rows = every[:, :, : reach * tile_units].reshape(nctx, tiles, reach, tile_units, PANEL)
    filter_sum = lag_rows.transpose(2, 4, 0, 1, 3).reshape(filter_len, groups)
    filter_grad = jnp.where(keep, filter_sum, jnp.zeros((), jnp.float32))
    short_rows = every[:, :, reach * tile_units : reach * tile_units + 9]
    short_grad = short_rows.transpose(2, 0, 1, 3).reshape(3, 3, channels)
    return (layer_out[None], input_grad[None], filter_grad, short_grad)


def solution(mesh):
    return jax.shard_map(
        functools.partial(shards, mesh.shape["dp"], mesh.shape["ctx"]),
        mesh=mesh,
        in_specs=(P("dp", "ctx", None), P(), P(), P(), P("dp", "ctx", None)),
        out_specs=(P("dp", "ctx", None), P("dp", "ctx", None), P(), P()),
        check_vma=False,
    )
```

```python
import functools

import jax
import jax.numpy as jnp
from jax import lax
from jax.experimental import pallas as pl
from jax.experimental.pallas import tpu as pltpu
from jax.sharding import PartitionSpec as P

PANEL = 128
UNIT = 16
TILE = 128
TAPS = 3
UNROLL = 4
MESH = pl.DeviceIdType.MESH


def rows_down(x, rows):
    return jnp.concatenate([jnp.zeros((rows, x.shape[1]), x.dtype), x[:-rows]], axis=0)


def rows_up(x, rows):
    return jnp.concatenate([x[rows:], jnp.zeros((rows, x.shape[1]), x.dtype)], axis=0)


def causal():
    shape = (PANEL, PANEL)
    return lax.broadcasted_iota(jnp.int32, shape, 1) >= lax.broadcasted_iota(jnp.int32, shape, 0)


def toeplitz(taps):
    width = taps.shape[1]
    x = jnp.broadcast_to(taps, (8, width))
    row = lax.broadcasted_iota(jnp.int32, (8, width), 0)
    for bit in (1, 2, 4):
        x = jnp.where((row & bit) != 0, pltpu.roll(x, bit, 1), x)
    rows = 8
    while rows < PANEL:
        x = jnp.concatenate([x, pltpu.roll(x, rows, 1)], axis=0)
        rows *= 2
    first = jnp.where(causal(), x[:, :PANEL], 0.0)
    return jnp.concatenate([first, x[:, PANEL:]], axis=1).astype(jnp.bfloat16)


def lag_sums(products):
    width = products.shape[1]
    first = jnp.where(causal(), products[:, :PANEL], 0.0)
    x = jnp.concatenate([first, products[:, PANEL:]], axis=1)
    rows = PANEL // 2
    while rows >= 8:
        x = x[:rows] + pltpu.roll(x[rows:], width - rows, 1)
        rows //= 2
    for step in (4, 2, 1):
        x = x + pltpu.roll(pltpu.roll(x, 8 - step, 0), width - step, 1)
    return x[0:1]


def tile_terms(reach, panels, ft, ct, wt, spreads, out_t, in_t, fg, sg_t):
    rows = panels * UNIT

    def group(g, carry):
        first = pl.multiple_of(g * UNIT, UNIT)
        lane = lax.broadcasted_iota(jnp.int32, (rows, PANEL), 1)
        chan = pl.ds(first, UNIT)
        feat = ft[:, chan, :].reshape(rows, PANEL)
        cot = ct[:, chan, :].reshape(rows, PANEL)
        w_all = wt[chan, :]

        def weigh(k, x):
            w = jnp.broadcast_to(w_all[:, k : k + 1], (UNIT, PANEL))
            return (x.reshape(panels, UNIT, PANEL) * w[None]).reshape(rows, PANEL)

        feats = [feat]
        for tap in range(1, TAPS):
            turned = pltpu.roll(feat, tap, 1)
            feats.append(jnp.where(lane < tap, rows_down(turned, UNIT), turned))
        streams = []
        for m in range(3):
            total = weigh(m * TAPS, feats[0])
            for tap in range(1, TAPS):
                total = total + weigh(m * TAPS + tap, feats[tap])
            streams.append(total)
        query, key, value = streams
        mixed = (key * value).astype(jnp.bfloat16)
        grad_conv = (cot * query).astype(jnp.bfloat16)
        earlier = jnp.concatenate(
            [mixed] + [rows_down(mixed, o * UNIT) for o in range(1, reach)], axis=1
        )
        later = jnp.concatenate(
            [grad_conv] + [rows_up(grad_conv, o * UNIT) for o in range(1, reach)], axis=1
        )
        spread = spreads[g]
        stacked = jnp.concatenate(
            [spread[:, o * PANEL : (o + 1) * PANEL] for o in range(reach)], axis=0
        )
        conv = jnp.dot(earlier, stacked, preferred_element_type=jnp.float32)
        back = lax.dot_general(
            later, spread, (((1,), (1,)), ((), ())), preferred_element_type=jnp.float32
        )
        products = lax.dot_general(
            mixed, later, (((0,), (0,)), ((), ())), preferred_element_type=jnp.float32
        )
        fg[pl.ds(g, 1), :] = lag_sums(products)
        out_t[:, chan, :] = (query * conv).reshape(panels, UNIT, PANEL)
        grads = (cot * conv, back * value, back * key)
        grad_in = None
        for tap in range(TAPS):
            part = weigh(tap, grads[0]) + weigh(TAPS + tap, grads[1]) + weigh(2 * TAPS + tap, grads[2])
            if tap:
                turned = pltpu.roll(part, PANEL - tap, 1)
                part = jnp.where(lane >= PANEL - tap, rows_up(turned, UNIT), turned)
            grad_in = part if grad_in is None else grad_in + part
        in_t[:, chan, :] = grad_in.reshape(panels, UNIT, PANEL)
        small_lane = lax.broadcasted_iota(jnp.int32, (UNIT, PANEL), 1)
        sums = jnp.zeros((UNIT, PANEL), jnp.float32)
        for m in range(3):
            for tap in range(TAPS):
                part = jnp.sum((grads[m] * feats[tap]).reshape(panels, UNIT, PANEL), axis=0)
                sums = jnp.where(small_lane == m * TAPS + tap, jnp.sum(part, axis=1, keepdims=True), sums)
        sg_t[chan, :] = sums
        return carry

    lax.fori_loop(0, TILE // UNIT, group, 0, unroll=UNROLL)


def layer_kernel(
    reach, ndp, nctx, f_hbm, c_hbm, wt, taps, out_hbm, in_hbm, all_hbm,
    arrived, leaving, spreads, ft, ct, out_t, in_t, fg, sg_t, pay, parts, sums,
    own_sem, in_send, in_recv, out_send, out_recv, keep_sem,
    rs_send, rs_recv, gd_send, gd_recv, gd_own, gc_send, gc_recv,
):
    dp, me = lax.axis_index("dp"), lax.axis_index("ctx")
    width = arrived.shape[3]
    tiles = width // TILE
    chunk = sums.shape[1]
    ins, outs = (f_hbm, c_hbm), (out_hbm, in_hbm)

    def ctx_peer(k):
        return lax.rem(me + k, nctx)

    def dp_peer(k):
        return lax.rem(dp + k, ndp)

    def lanes(j):
        return pl.ds(pl.multiple_of(j * TILE, TILE), TILE)

    def cols(owner, j):
        return pl.ds(pl.multiple_of(owner * width + j * TILE, TILE), TILE)

    def copy(src, dst, send, recv, device):
        return pltpu.make_async_remote_copy(
            src_ref=src, dst_ref=dst, send_sem=send, recv_sem=recv, device_id=device, device_id_type=MESH
        )

    def in_copy(a, j, k, slot):
        return copy(
            ins[a].at[:, cols(ctx_peer(k), j)],
            arrived.at[a, slot, :, lanes(j)],
            in_send.at[a, j, k],
            in_recv.at[a, j, k],
            (dp, ctx_peer(k)),
        )

    def in_own(a, j):
        return pltpu.make_async_copy(
            ins[a].at[:, cols(me, j)], arrived.at[a, me, :, lanes(j)], own_sem.at[a, j]
        )

    def out_copy(a, j, k, slot):
        return copy(
            leaving.at[a, ctx_peer(k), :, lanes(j)],
            outs[a].at[:, cols(slot, j)],
            out_send.at[a, j, k],
            out_recv.at[a, j, k],
            (dp, ctx_peer(k)),
        )

    def out_own(a, j):
        return pltpu.make_async_copy(
            leaving.at[a, me, :, lanes(j)], outs[a].at[:, cols(me, j)], keep_sem.at[a, j]
        )

    def rs_copy(j, k):
        return copy(
            pay.at[j, dp_peer(k)], parts.at[j, k], rs_send.at[j, k], rs_recv.at[j, k], (dp_peer(k), me)
        )

    def gc_copy(j, k, slot):
        return copy(
            sums.at[j], all_hbm.at[j, dp, slot], gc_send.at[j, k], gc_recv.at[j, k], (dp, ctx_peer(k))
        )

    def gc_keep(j):
        return pltpu.make_async_copy(sums.at[j], all_hbm.at[j, dp, me], gd_own.at[j])

    def gd_copy(j, k, slot):
        return copy(
            all_hbm.at[j, dp], all_hbm.at[j, slot], gd_send.at[j, k], gd_recv.at[j, k], (dp_peer(k), me)
        )

    def each(count, body, unroll=1):
        def step(i, carry):
            body(i)
            return carry

        lax.fori_loop(0, count, step, 0, unroll=unroll)

    barrier = pltpu.get_barrier_semaphore()
    for k in range(1, nctx):
        pl.semaphore_signal(barrier, inc=1, device_id=(dp, ctx_peer(k)), device_id_type=MESH)
    for k in range(1, ndp):
        pl.semaphore_signal(barrier, inc=1, device_id=(dp_peer(k), me), device_id_type=MESH)
    for a in range(2):
        each(tiles, lambda j: in_own(a, j).start())
    pl.semaphore_wait(barrier, nctx + ndp - 2)

    def send_in(j):
        for a in range(2):
            each(nctx - 1, lambda i: in_copy(a, j, i + 1, me).start())

    each(tiles, send_in)

    def build(g):
        spreads[g] = toeplitz(taps[pl.ds(g, 1), :])

    each(taps.shape[0], build, UNROLL)

    def spread_ctx(j):
        each(ndp - 1, lambda i: rs_copy(j, i + 1).wait_recv())
        total = pay[j, dp]
        for k in range(1, ndp):
            total = total + parts[j, k]
        sums[j] = total.astype(jnp.bfloat16)
        gc_keep(j).start()
        each(nctx - 1, lambda i: gc_copy(j, i + 1, me).start())

    def spread_dp(j):
        gc_keep(j).wait()
        each(nctx - 1, lambda i: gc_copy(j, i + 1, lax.rem(me + nctx - i - 1, nctx)).wait_recv())
        each(ndp - 1, lambda i: gd_copy(j, i + 1, dp).start())

    def one_tile(j):
        for a in range(2):
            in_own(a, j).wait()
            each(
                nctx - 1,
                lambda i: in_copy(a, j, i + 1, lax.rem(me + nctx - i - 1, nctx)).wait_recv(),
            )

        def turn_in(n):
            ft[n] = arrived[0, n, :, lanes(j)].astype(jnp.float32).T
            ct[n] = arrived[1, n, :, lanes(j)].astype(jnp.float32).T

        each(nctx, turn_in, UNROLL)
        units = TILE // UNIT
        tile_terms(
            reach, nctx, ft, ct, wt.at[lanes(j), :],
            spreads.at[pl.ds(j * units, units)], out_t, in_t, fg, sg_t,
        )

        def turn_out(n):
            leaving[0, n, :, lanes(j)] = out_t[n].T.astype(jnp.bfloat16)
            leaving[1, n, :, lanes(j)] = in_t[n].T.astype(jnp.bfloat16)

        each(nctx, turn_out, UNROLL)
        rows = [fg[:, o * PANEL : (o + 1) * PANEL] for o in range(reach)] + [sg_t[...].T[:UNIT]]
        filled = reach * units + UNIT
        if filled < ndp * chunk:
            rows.append(jnp.zeros((ndp * chunk - filled, PANEL), jnp.float32))
        pay[j] = jnp.concatenate(rows, axis=0).reshape(ndp, chunk, PANEL)
        each(ndp - 1, lambda i: rs_copy(j, i + 1).start())
        for a in range(2):
            out_own(a, j).start()
            each(nctx - 1, lambda i: out_copy(a, j, i + 1, me).start())

        @pl.when(j >= 1)
        def _():
            spread_ctx(j - 1)

        @pl.when(j >= 2)
        def _():
            spread_dp(j - 2)

    each(tiles, one_tile)
    if tiles >= 2:
        spread_dp(tiles - 2)
    spread_ctx(tiles - 1)
    spread_dp(tiles - 1)

    def finish(j):
        for a in range(2):
            each(nctx - 1, lambda i: in_copy(a, j, i + 1, me).wait_send())
            out_own(a, j).wait()
            each(nctx - 1, lambda i: out_copy(a, j, i + 1, me).wait_send())
            each(
                nctx - 1,
                lambda i: out_copy(a, j, i + 1, lax.rem(me + nctx - i - 1, nctx)).wait_recv(),
            )
        each(ndp - 1, lambda i: rs_copy(j, i + 1).wait_send())
        each(nctx - 1, lambda i: gc_copy(j, i + 1, me).wait_send())
        each(ndp - 1, lambda i: gd_copy(j, i + 1, dp).wait_send())
        each(ndp - 1, lambda i: gd_copy(j, i + 1, lax.rem(dp + ndp - i - 1, ndp)).wait_recv())

    each(tiles, finish)


def shards(ndp, nctx, features, short_weights, filters, reach_panels, cotangent):
    filter_len, groups = filters.shape
    channels = features.shape[2]
    reach = filter_len // PANEL
    lag_pos = lax.broadcasted_iota(jnp.int32, (filter_len, groups), 0)
    keep = lag_pos < reach_panels[None, :] * PANEL
    masked = jnp.where(keep, filters, jnp.zeros((), filters.dtype))
    rows = features.shape[1]
    assert rows == PANEL and features.shape[0] == 1
    width = channels // nctx
    tiles = width // TILE
    me = lax.axis_index("ctx")
    units = width // UNIT
    tile_units = TILE // UNIT
    taps = lax.dynamic_slice_in_dim(masked, me * units, units, 1).T.astype(jnp.float32)
    wt = lax.dynamic_slice_in_dim(short_weights.reshape(9, channels), me * width, width, 1).T
    filled = reach * tile_units + UNIT
    chunk = -(-filled // (UNIT * ndp)) * UNIT
    hbm = pl.BlockSpec(memory_space=pltpu.HBM)
    vmem = pl.BlockSpec(memory_space=pltpu.VMEM)
    dma = pltpu.SemaphoreType.DMA
    turned = pltpu.VMEM((nctx, TILE, PANEL), jnp.float32)
    layer_out, input_grad, every = pl.pallas_call(
        functools.partial(layer_kernel, reach, ndp, nctx),
        in_specs=[hbm, hbm, vmem, vmem],
        out_specs=[hbm, hbm, hbm],
        out_shape=[
            jax.ShapeDtypeStruct((rows, channels), jnp.bfloat16),
            jax.ShapeDtypeStruct((rows, channels), jnp.bfloat16),
            jax.ShapeDtypeStruct((tiles, ndp, nctx, chunk, PANEL), jnp.bfloat16),
        ],
        scratch_shapes=[
            pltpu.VMEM((2, nctx, PANEL, width), jnp.bfloat16),
            pltpu.VMEM((2, nctx, PANEL, width), jnp.bfloat16),
            pltpu.VMEM((units, PANEL, filter_len), jnp.bfloat16),
            turned,
            turned,
            turned,
            turned,
            pltpu.VMEM((tile_units, filter_len), jnp.float32),
            pltpu.VMEM((TILE, PANEL), jnp.float32),
            pltpu.VMEM((tiles, ndp, chunk, PANEL), jnp.float32),
            pltpu.VMEM((tiles, ndp, chunk, PANEL), jnp.float32),
            pltpu.VMEM((tiles, chunk, PANEL), jnp.bfloat16),
            dma((2, tiles)),
            dma((2, tiles, nctx)),
            dma((2, tiles, nctx)),
            dma((2, tiles, nctx)),
            dma((2, tiles, nctx)),
            dma((2, tiles)),
            dma((tiles, ndp)),
            dma((tiles, ndp)),
            dma((tiles, ndp)),
            dma((tiles, ndp)),
            dma((tiles,)),
            dma((tiles, nctx)),
            dma((tiles, nctx)),
        ],
        compiler_params=pltpu.CompilerParams(
            collective_id=0, has_side_effects=True, vmem_limit_bytes=40 * 2**20
        ),
    )(features[0], cotangent[0], wt, taps)
    every = every.astype(jnp.float32).transpose(2, 0, 1, 3, 4).reshape(nctx, tiles, ndp * chunk, PANEL)
    lag_rows = every[:, :, : reach * tile_units].reshape(nctx, tiles, reach, tile_units, PANEL)
    filter_sum = lag_rows.transpose(2, 4, 0, 1, 3).reshape(filter_len, groups)
    filter_grad = jnp.where(keep, filter_sum, jnp.zeros((), jnp.float32))
    short_rows = every[:, :, reach * tile_units : reach * tile_units + 9]
    short_grad = short_rows.transpose(2, 0, 1, 3).reshape(3, 3, channels)
    return (layer_out[None], input_grad[None], filter_grad, short_grad)


def solution(mesh):
    return jax.shard_map(
        functools.partial(shards, mesh.shape["dp"], mesh.shape["ctx"]),
        mesh=mesh,
        in_specs=(P("dp", "ctx", None), P(), P(), P(), P("dp", "ctx", None)),
        out_specs=(P("dp", "ctx", None), P("dp", "ctx", None), P(), P()),
        check_vma=False,
    )
```

```python
import functools

import jax
import jax.numpy as jnp
from jax import lax
from jax.experimental import pallas as pl
from jax.experimental.pallas import tpu as pltpu
from jax.sharding import PartitionSpec as P

PANEL = 128
UNIT = 16
TILE = 128
TAPS = 3
UNROLL = 4
MESH = pl.DeviceIdType.MESH


def rows_down(x, rows):
    return jnp.concatenate([jnp.zeros((rows, x.shape[1]), x.dtype), x[:-rows]], axis=0)


def rows_up(x, rows):
    return jnp.concatenate([x[rows:], jnp.zeros((rows, x.shape[1]), x.dtype)], axis=0)


def causal():
    shape = (PANEL, PANEL)
    return lax.broadcasted_iota(jnp.int32, shape, 1) >= lax.broadcasted_iota(jnp.int32, shape, 0)


def toeplitz(taps):
    width = taps.shape[1]
    x = jnp.broadcast_to(taps, (8, width))
    row = lax.broadcasted_iota(jnp.int32, (8, width), 0)
    for bit in (1, 2, 4):
        x = jnp.where((row & bit) != 0, pltpu.roll(x, bit, 1), x)
    rows = 8
    while rows < PANEL:
        x = jnp.concatenate([x, pltpu.roll(x, rows, 1)], axis=0)
        rows *= 2
    first = jnp.where(causal(), x[:, :PANEL], 0.0)
    return jnp.concatenate([first, x[:, PANEL:]], axis=1).astype(jnp.bfloat16)


def lag_sums(products):
    width = products.shape[1]
    first = jnp.where(causal(), products[:, :PANEL], 0.0)
    x = jnp.concatenate([first, products[:, PANEL:]], axis=1)
    rows = PANEL // 2
    while rows >= 8:
        x = x[:rows] + pltpu.roll(x[rows:], width - rows, 1)
        rows //= 2
    for step in (4, 2, 1):
        x = x + pltpu.roll(pltpu.roll(x, 8 - step, 0), width - step, 1)
    return x[0:1]


def tile_terms(reach, panels, ft, ct, wt, spreads, out_t, in_t, fg, sg_t):
    rows = panels * UNIT

    def group(g, carry):
        first = pl.multiple_of(g * UNIT, UNIT)
        lane = lax.broadcasted_iota(jnp.int32, (rows, PANEL), 1)
        chan = pl.ds(first, UNIT)
        feat = ft[:, chan, :].reshape(rows, PANEL)
        cot = ct[:, chan, :].reshape(rows, PANEL)
        w_all = wt[chan, :]

        def weigh(k, x):
            w = jnp.broadcast_to(w_all[:, k : k + 1], (UNIT, PANEL))
            return (x.reshape(panels, UNIT, PANEL) * w[None]).reshape(rows, PANEL)

        feats = [feat]
        for tap in range(1, TAPS):
            turned = pltpu.roll(feat, tap, 1)
            feats.append(jnp.where(lane < tap, rows_down(turned, UNIT), turned))
        streams = []
        for m in range(3):
            total = weigh(m * TAPS, feats[0])
            for tap in range(1, TAPS):
                total = total + weigh(m * TAPS + tap, feats[tap])
            streams.append(total)
        query, key, value = streams
        mixed = (key * value).astype(jnp.bfloat16)
        grad_conv = (cot * query).astype(jnp.bfloat16)
        earlier = jnp.concatenate(
            [mixed] + [rows_down(mixed, o * UNIT) for o in range(1, reach)], axis=1
        )
        later = jnp.concatenate(
            [grad_conv] + [rows_up(grad_conv, o * UNIT) for o in range(1, reach)], axis=1
        )
        spread = spreads[g]
        stacked = jnp.concatenate(
            [spread[:, o * PANEL : (o + 1) * PANEL] for o in range(reach)], axis=0
        )
        conv = jnp.dot(earlier, stacked, preferred_element_type=jnp.float32)
        back = lax.dot_general(
            later, spread, (((1,), (1,)), ((), ())), preferred_element_type=jnp.float32
        )
        products = lax.dot_general(
            mixed, later, (((0,), (0,)), ((), ())), preferred_element_type=jnp.float32
        )
        fg[pl.ds(g, 1), :] = lag_sums(products)
        out_t[:, chan, :] = (query * conv).reshape(panels, UNIT, PANEL)
        grads = (cot * conv, back * value, back * key)
        grad_in = None
        for tap in range(TAPS):
            part = weigh(tap, grads[0]) + weigh(TAPS + tap, grads[1]) + weigh(2 * TAPS + tap, grads[2])
            if tap:
                turned = pltpu.roll(part, PANEL - tap, 1)
                part = jnp.where(lane >= PANEL - tap, rows_up(turned, UNIT), turned)
            grad_in = part if grad_in is None else grad_in + part
        in_t[:, chan, :] = grad_in.reshape(panels, UNIT, PANEL)
        small_lane = lax.broadcasted_iota(jnp.int32, (UNIT, PANEL), 1)
        sums = jnp.zeros((UNIT, PANEL), jnp.float32)
        for m in range(3):
            for tap in range(TAPS):
                part = jnp.sum((grads[m] * feats[tap]).reshape(panels, UNIT, PANEL), axis=0)
                sums = jnp.where(small_lane == m * TAPS + tap, jnp.sum(part, axis=1, keepdims=True), sums)
        sg_t[chan, :] = sums
        return carry

    lax.fori_loop(0, TILE // UNIT, group, 0, unroll=UNROLL)


def layer_kernel(
    reach, ndp, nctx, f_hbm, c_hbm, wt, taps, out_hbm, in_hbm, all_hbm,
    arrived, leaving, spreads, ft, ct, out_t, in_t, fg, sg_t, pay, parts, sums,
    own_sem, in_send, in_recv, out_send, out_recv, keep_sem,
    rs_send, rs_recv, gd_send, gd_recv, gd_own, gc_send, gc_recv,
):
    dp, me = lax.axis_index("dp"), lax.axis_index("ctx")
    width = arrived.shape[3]
    tiles = width // TILE
    chunk = sums.shape[1]
    ins, outs = (f_hbm, c_hbm), (out_hbm, in_hbm)

    def ctx_peer(k):
        return lax.rem(me + k, nctx)

    def dp_peer(k):
        return lax.rem(dp + k, ndp)

    def lanes(j):
        return pl.ds(pl.multiple_of(j * TILE, TILE), TILE)

    def cols(owner, j):
        return pl.ds(pl.multiple_of(owner * width + j * TILE, TILE), TILE)

    def copy(src, dst, send, recv, device):
        return pltpu.make_async_remote_copy(
            src_ref=src, dst_ref=dst, send_sem=send, recv_sem=recv, device_id=device, device_id_type=MESH
        )

    def in_copy(a, j, k, slot):
        return copy(
            ins[a].at[:, cols(ctx_peer(k), j)],
            arrived.at[a, slot, :, lanes(j)],
            in_send.at[a, j, k],
            in_recv.at[a, j, k],
            (dp, ctx_peer(k)),
        )

    def in_own(a, j):
        return pltpu.make_async_copy(
            ins[a].at[:, cols(me, j)], arrived.at[a, me, :, lanes(j)], own_sem.at[a, j]
        )

    def out_copy(a, j, k, slot):
        return copy(
            leaving.at[a, ctx_peer(k), :, lanes(j)],
            outs[a].at[:, cols(slot, j)],
            out_send.at[a, j, k],
            out_recv.at[a, j, k],
            (dp, ctx_peer(k)),
        )

    def out_own(a, j):
        return pltpu.make_async_copy(
            leaving.at[a, me, :, lanes(j)], outs[a].at[:, cols(me, j)], keep_sem.at[a, j]
        )

    def rs_copy(j, k):
        return copy(
            pay.at[j, dp_peer(k)], parts.at[j, k], rs_send.at[j, k], rs_recv.at[j, k], (dp_peer(k), me)
        )

    def gc_copy(j, k, slot):
        return copy(
            sums.at[j], all_hbm.at[j, dp, slot], gc_send.at[j, k], gc_recv.at[j, k], (dp, ctx_peer(k))
        )

    def gc_keep(j):
        return pltpu.make_async_copy(sums.at[j], all_hbm.at[j, dp, me], gd_own.at[j])

    def gd_copy(j, k, slot):
        return copy(
            all_hbm.at[j, dp], all_hbm.at[j, slot], gd_send.at[j, k], gd_recv.at[j, k], (dp_peer(k), me)
        )

    def each(count, body, unroll=1):
        def step(i, carry):
            body(i)
            return carry

        lax.fori_loop(0, count, step, 0, unroll=unroll)

    barrier = pltpu.get_barrier_semaphore()
    for k in range(1, nctx):
        pl.semaphore_signal(barrier, inc=1, device_id=(dp, ctx_peer(k)), device_id_type=MESH)
    for k in range(1, ndp):
        pl.semaphore_signal(barrier, inc=1, device_id=(dp_peer(k), me), device_id_type=MESH)
    for a in range(2):
        each(tiles, lambda j: in_own(a, j).start())
    pl.semaphore_wait(barrier, nctx + ndp - 2)

    def send_in(j):
        for a in range(2):
            each(nctx - 1, lambda i: in_copy(a, j, i + 1, me).start())

    ahead = min(2, tiles)
    each(ahead, send_in)

    def build(g):
        spreads[g] = toeplitz(taps[pl.ds(g, 1), :])

    each(taps.shape[0], build, UNROLL)

    def spread_ctx(j):
        each(ndp - 1, lambda i: rs_copy(j, i + 1).wait_recv())
        total = pay[j, dp]
        for k in range(1, ndp):
            total = total + parts[j, k]
        sums[j] = total.astype(jnp.bfloat16)
        gc_keep(j).start()
        each(nctx - 1, lambda i: gc_copy(j, i + 1, me).start())

    def spread_dp(j):
        gc_keep(j).wait()
        each(nctx - 1, lambda i: gc_copy(j, i + 1, lax.rem(me + nctx - i - 1, nctx)).wait_recv())
        each(ndp - 1, lambda i: gd_copy(j, i + 1, dp).start())

    def one_tile(j):
        for a in range(2):
            in_own(a, j).wait()
            each(
                nctx - 1,
                lambda i: in_copy(a, j, i + 1, lax.rem(me + nctx - i - 1, nctx)).wait_recv(),
            )

        @pl.when(j + ahead < tiles)
        def _():
            send_in(j + ahead)

        def turn_in(n):
            ft[n] = arrived[0, n, :, lanes(j)].astype(jnp.float32).T
            ct[n] = arrived[1, n, :, lanes(j)].astype(jnp.float32).T

        each(nctx, turn_in, UNROLL)
        units = TILE // UNIT
        tile_terms(
            reach, nctx, ft, ct, wt.at[lanes(j), :],
            spreads.at[pl.ds(j * units, units)], out_t, in_t, fg, sg_t,
        )

        def turn_out(n):
            leaving[0, n, :, lanes(j)] = out_t[n].T.astype(jnp.bfloat16)
            leaving[1, n, :, lanes(j)] = in_t[n].T.astype(jnp.bfloat16)

        each(nctx, turn_out, UNROLL)
        rows = [fg[:, o * PANEL : (o + 1) * PANEL] for o in range(reach)] + [sg_t[...].T[:UNIT]]
        filled = reach * units + UNIT
        if filled < ndp * chunk:
            rows.append(jnp.zeros((ndp * chunk - filled, PANEL), jnp.float32))
        pay[j] = jnp.concatenate(rows, axis=0).reshape(ndp, chunk, PANEL)
        each(ndp - 1, lambda i: rs_copy(j, i + 1).start())
        for a in range(2):
            out_own(a, j).start()
            each(nctx - 1, lambda i: out_copy(a, j, i + 1, me).start())

        @pl.when(j >= 1)
        def _():
            spread_ctx(j - 1)

        @pl.when(j >= 2)
        def _():
            spread_dp(j - 2)

    each(tiles, one_tile)
    if tiles >= 2:
        spread_dp(tiles - 2)
    spread_ctx(tiles - 1)
    spread_dp(tiles - 1)

    def finish(j):
        for a in range(2):
            each(nctx - 1, lambda i: in_copy(a, j, i + 1, me).wait_send())
            out_own(a, j).wait()
            each(nctx - 1, lambda i: out_copy(a, j, i + 1, me).wait_send())
            each(
                nctx - 1,
                lambda i: out_copy(a, j, i + 1, lax.rem(me + nctx - i - 1, nctx)).wait_recv(),
            )
        each(ndp - 1, lambda i: rs_copy(j, i + 1).wait_send())
        each(nctx - 1, lambda i: gc_copy(j, i + 1, me).wait_send())
        each(ndp - 1, lambda i: gd_copy(j, i + 1, dp).wait_send())
        each(ndp - 1, lambda i: gd_copy(j, i + 1, lax.rem(dp + ndp - i - 1, ndp)).wait_recv())

    each(tiles, finish)


def shards(ndp, nctx, features, short_weights, filters, reach_panels, cotangent):
    filter_len, groups = filters.shape
    channels = features.shape[2]
    reach = filter_len // PANEL
    lag_pos = lax.broadcasted_iota(jnp.int32, (filter_len, groups), 0)
    keep = lag_pos < reach_panels[None, :] * PANEL
    masked = jnp.where(keep, filters, jnp.zeros((), filters.dtype))
    rows = features.shape[1]
    assert rows == PANEL and features.shape[0] == 1
    width = channels // nctx
    tiles = width // TILE
    me = lax.axis_index("ctx")
    units = width // UNIT
    tile_units = TILE // UNIT
    taps = lax.dynamic_slice_in_dim(masked, me * units, units, 1).T.astype(jnp.float32)
    wt = lax.dynamic_slice_in_dim(short_weights.reshape(9, channels), me * width, width, 1).T
    filled = reach * tile_units + UNIT
    chunk = -(-filled // (UNIT * ndp)) * UNIT
    hbm = pl.BlockSpec(memory_space=pltpu.HBM)
    vmem = pl.BlockSpec(memory_space=pltpu.VMEM)
    dma = pltpu.SemaphoreType.DMA
    turned = pltpu.VMEM((nctx, TILE, PANEL), jnp.float32)
    layer_out, input_grad, every = pl.pallas_call(
        functools.partial(layer_kernel, reach, ndp, nctx),
        in_specs=[hbm, hbm, vmem, vmem],
        out_specs=[hbm, hbm, hbm],
        out_shape=[
            jax.ShapeDtypeStruct((rows, channels), jnp.bfloat16),
            jax.ShapeDtypeStruct((rows, channels), jnp.bfloat16),
            jax.ShapeDtypeStruct((tiles, ndp, nctx, chunk, PANEL), jnp.bfloat16),
        ],
        scratch_shapes=[
            pltpu.VMEM((2, nctx, PANEL, width), jnp.bfloat16),
            pltpu.VMEM((2, nctx, PANEL, width), jnp.bfloat16),
            pltpu.VMEM((units, PANEL, filter_len), jnp.bfloat16),
            turned,
            turned,
            turned,
            turned,
            pltpu.VMEM((tile_units, filter_len), jnp.float32),
            pltpu.VMEM((TILE, PANEL), jnp.float32),
            pltpu.VMEM((tiles, ndp, chunk, PANEL), jnp.float32),
            pltpu.VMEM((tiles, ndp, chunk, PANEL), jnp.float32),
            pltpu.VMEM((tiles, chunk, PANEL), jnp.bfloat16),
            dma((2, tiles)),
            dma((2, tiles, nctx)),
            dma((2, tiles, nctx)),
            dma((2, tiles, nctx)),
            dma((2, tiles, nctx)),
            dma((2, tiles)),
            dma((tiles, ndp)),
            dma((tiles, ndp)),
            dma((tiles, ndp)),
            dma((tiles, ndp)),
            dma((tiles,)),
            dma((tiles, nctx)),
            dma((tiles, nctx)),
        ],
        compiler_params=pltpu.CompilerParams(
            collective_id=0, has_side_effects=True, vmem_limit_bytes=40 * 2**20
        ),
    )(features[0], cotangent[0], wt, taps)
    every = every.astype(jnp.float32).transpose(2, 0, 1, 3, 4).reshape(nctx, tiles, ndp * chunk, PANEL)
    lag_rows = every[:, :, : reach * tile_units].reshape(nctx, tiles, reach, tile_units, PANEL)
    filter_sum = lag_rows.transpose(2, 4, 0, 1, 3).reshape(filter_len, groups)
    filter_grad = jnp.where(keep, filter_sum, jnp.zeros((), jnp.float32))
    short_rows = every[:, :, reach * tile_units : reach * tile_units + 9]
    short_grad = short_rows.transpose(2, 0, 1, 3).reshape(3, 3, channels)
    return (layer_out[None], input_grad[None], filter_grad, short_grad)


def solution(mesh):
    return jax.shard_map(
        functools.partial(shards, mesh.shape["dp"], mesh.shape["ctx"]),
        mesh=mesh,
        in_specs=(P("dp", "ctx", None), P(), P(), P(), P("dp", "ctx", None)),
        out_specs=(P("dp", "ctx", None), P("dp", "ctx", None), P(), P()),
        check_vma=False,
    )
```
